32 devices in a mesh: az: 16 (over z, x, core), dep: 2 (over y).
Axes of the slice: x: 2, y: 2, z: 4, core: 2. Of those that a mesh axis runs over, the one named last changes fastest.
Arguments:
- field: float32 [1024, 2, 1024], P('az', None, 'dep'), may hold values from -6 to 6
- brick_speed: bfloat16 [4096, 1024], P('az', 'dep'), may hold values from -40 to 40
- send_index: int32 [16, 16, 32], P('az'), may hold values from 0 to 255
- send_count: int32 [16, 16], P('az'), may hold values from 0 to 32, as said below
- weights: bfloat16 [1024, 4, 512], P('az'), may hold values from 0 to 1, as said below
- propagator: bfloat16 [2, 2, 1024, 1024], replicated, may hold values from -1 to 1
Outputs:
- pressure: float32 [1024, 2, 1024], P('az', None, 'dep')
The draws below stay inside these ranges and needn't reach their ends.
Inputs may be any that keep to these rules, and one draw needn't show every extreme that they name: `send_count`: 32 or fewer columns from one brick to one sector; one sector receives 32 from every brick. Nonnegative interpolation weights.
All inputs are finite; a program needn't handle non-finite values.
Results may differ from the reference program's by a relative error of at most 0.025.
Values may be sent and summed in bfloat16 or wider, within the bound.
A program may use at most 64 MiB of HBM per device.

```python
import jax
import jax.numpy as jnp
from jax import lax

NZ = 1024
AZ_DEV = 64
BCOL = 256
CAP = 32
NSTEP = 4
NPADE = 2
SECTORS = 16
AZ = 1024


def intersection_counts(key):
    inner = jax.random.fold_in(key, 11)
    first, second = jax.random.split(inner)
    base = jax.random.randint(first, (SECTORS, SECTORS), 0, CAP + 1)
    busiest = jax.random.randint(second, (), 0, SECTORS)
    column = lax.broadcasted_iota(jnp.int32, (SECTORS, SECTORS), 1)
    return jnp.where(column == busiest, CAP, base).astype(jnp.int32)


def draw_send_count(key, part):
    return intersection_counts(key)


def draw_weights(key, part):
    inner = jax.random.fold_in(key, 23)
    first, second = jax.random.split(inner)
    picked = jax.random.randint(first, (AZ, NSTEP, SECTORS * CAP), 0, SECTORS * CAP) < 32
    values = jax.random.uniform(second, (AZ, NSTEP, SECTORS * CAP), jnp.float32, 0.03, 0.1)
    return jnp.where(picked, values, 0.0).astype(jnp.bfloat16)


def draw_propagator(key, part):
    inner = jax.random.fold_in(key, 37)
    first, second = jax.random.split(inner)
    phase = jax.random.uniform(first, (NPADE, NZ), jnp.float32, -jnp.pi, jnp.pi)
    noise = jax.random.truncated_normal(second, -3.0, 3.0, (NPADE, 2, NZ, NZ), jnp.float32)
    noise = noise * (0.5 / NZ ** 0.5)
    rowid = lax.broadcasted_iota(jnp.int32, (NZ, NZ), 0)
    colid = lax.broadcasted_iota(jnp.int32, (NZ, NZ), 1)
    identity = (rowid == colid).astype(jnp.float32)
    diag_real = jnp.cos(phase)[:, :, None] * identity[None]
    diag_imag = jnp.sin(phase)[:, :, None] * identity[None]
    matrix = jnp.stack([diag_real, diag_imag], axis=1) + noise
    return (matrix / 1.5 ** 0.5).astype(jnp.bfloat16)


def touch_ends(values, own_key, least, largest):
    shape = values.shape
    spot = [jax.random.randint(jax.random.fold_in(own_key, axis), (), 0, shape[axis]) for axis in range(len(shape))]
    values = values.at[tuple(spot)].set(least)
    longest = shape.index(max(shape))
    spot[longest] = (spot[longest] + 1) % shape[longest]
    return values.at[tuple(spot)].set(largest)


def steps_of(own_key, shape, cuts, least, largest):
    gain = 1.0
    for dim, blocks in cuts:
        steps = jax.random.uniform(jax.random.fold_in(jax.random.fold_in(own_key, 6), dim), (blocks,), jnp.float32, least / len(cuts), largest / len(cuts))
        gain = gain * jnp.repeat(jnp.exp(steps), shape[dim] // blocks).reshape((-1,) + (1,) * (len(shape) - 1 - dim))
    return gain


def gaussian(stream_key, shape, scale, bound, pieces=(), kind=jnp.bfloat16):
    gain = steps_of(stream_key, shape, pieces, -0.22, 0.18) if pieces else 1.0
    drawn = jax.random.normal(stream_key, shape, jnp.float32) * scale * gain
    return jnp.minimum(jnp.maximum(drawn, -bound), bound).astype(kind)


def setup_inputs(seed: int = 0) -> dict:
    keys = jax.random.split(jax.random.key(seed), 7)
    field = gaussian(keys[0], (AZ, 2, NZ), 1.0, 6.0, ((0, 16), (2, 2)), jnp.float32)
    brick_speed = jnp.clip(jax.random.uniform(keys[1], (SECTORS * BCOL, NZ), jnp.float32, -40.0, 40.0) * steps_of(keys[1], (SECTORS * BCOL, NZ), ((0, 16), (1, 2)), -0.4, 0.0), -40.0, 40.0).astype(jnp.bfloat16)
    send_index = touch_ends(jax.random.randint(keys[2], (SECTORS, SECTORS, CAP), 0, BCOL), jax.random.fold_in(keys[2], 1), 0, BCOL - 1).astype(jnp.int32)
    send_count = draw_send_count(jax.random.fold_in(keys[6], 71), 0)
    weights = draw_weights(jax.random.fold_in(keys[6], 71), 0)
    propagator = draw_propagator(jax.random.fold_in(keys[6], 71), 0)
    return dict(field=field, brick_speed=brick_speed, send_index=send_index, send_count=send_count, weights=weights, propagator=propagator)


angle_rate = 200.0 / 1500.0
couple_real = 0.1
couple_imag = 0.15


def apply_screen(field, angle):
    cosine = jnp.cos(angle)
    sine = jnp.sin(angle)
    real_part = field[:, 0] * cosine - field[:, 1] * sine
    imag_part = field[:, 0] * sine + field[:, 1] * cosine
    return jnp.stack([real_part, imag_part], axis=1)


def azimuth_couple(padded, rows):
    laplace = (-padded[0:rows] + 16.0 * padded[1:rows + 1] - 30.0 * padded[2:rows + 2]
               + 16.0 * padded[3:rows + 3] - padded[4:rows + 4]) / 12.0
    centre = padded[2:rows + 2]
    real_part = centre[:, 0] + couple_real * laplace[:, 0] - couple_imag * laplace[:, 1]
    imag_part = centre[:, 1] + couple_real * laplace[:, 1] + couple_imag * laplace[:, 0]
    return jnp.stack([real_part, imag_part], axis=1)


def combine_parts(mixed):
    real_part = mixed[:, 0, 0] - mixed[:, 1, 1]
    imag_part = mixed[:, 0, 1] + mixed[:, 1, 0]
    return jnp.stack([real_part, imag_part], axis=1)


def reference(field, brick_speed, send_index, send_count, weights, propagator):
    offsets = (jnp.arange(SECTORS, dtype=jnp.int32) * BCOL)[:, None]

    def one_sector(sector):
        chosen = lax.dynamic_index_in_dim(send_index, sector, 1, keepdims=False)
        limit = lax.dynamic_index_in_dim(send_count, sector, 1, keepdims=False)
        received = brick_speed[chosen + offsets]
        slots = lax.broadcasted_iota(jnp.int32, chosen.shape, 1)
        keep = (slots < limit[:, None])[:, :, None]
        received = jnp.where(keep, received, jnp.zeros_like(received))
        block = lax.dynamic_slice_in_dim(weights, sector * AZ_DEV, AZ_DEV, 0)
        flat = received.reshape(SECTORS * CAP, NZ)
        return jnp.einsum('akm,mz->akz', block.astype(jnp.float32), flat.astype(jnp.float32))

    speed = lax.map(one_sector, jnp.arange(SECTORS, dtype=jnp.int32)).reshape(AZ, NSTEP, NZ)
    angle = -angle_rate * speed
    for step in range(NSTEP):
        field = apply_screen(field, angle[:, step, :])
        padded = jnp.concatenate([field[-2:], field, field[:2]], axis=0)
        field = azimuth_couple(padded, AZ)
        for factor in range(NPADE):
            rounded = lax.optimization_barrier(field.astype(jnp.bfloat16))
            mixed = jnp.einsum('acz,pzw->acpw', rounded.astype(jnp.float32),
                               propagator[factor].astype(jnp.float32))
            field = combine_parts(mixed)
    return field
```

```python
import functools
import math

import jax
import jax.numpy as jnp
from jax import lax
from jax.experimental import pallas as pl
from jax.experimental.pallas import tpu as pltpu
from jax.sharding import PartitionSpec as P

angle_rate = 200.0 / 1500.0
couple_real = 0.1
couple_imag = 0.15
MESH = pl.DeviceIdType.MESH
LANES = 128


def sine_cosine(x):
    turns = jnp.floor(x * (2.0 / math.pi) + 0.5)
    r = x - turns * 1.5703125
    r = r - turns * 4.837512969970703125e-4
    r = r - turns * 7.549789948768648e-8
    quadrant = turns.astype(jnp.int32)
    r2 = r * r
    sine = r + r * r2 * (-1.0 / 6.0 + r2 * (1.0 / 120.0 + r2 * (-1.0 / 5040.0)))
    cosine = 1.0 + r2 * (-0.5 + r2 * (1.0 / 24.0 + r2 * (-1.0 / 720.0 + r2 * (1.0 / 40320.0))))
    swap = (quadrant & 1) == 1
    out_sine = jnp.where(swap, cosine, sine)
    out_cosine = jnp.where(swap, sine, cosine)
    out_sine = jnp.where((quadrant & 2) == 2, -out_sine, out_sine)
    out_cosine = jnp.where(((quadrant + 1) & 2) == 2, -out_cosine, out_cosine)
    return out_sine, out_cosine


def march_kernel(
    n, steps, factors, cap, halo, half,
    field_hbm, brick_hbm, index_hbm, count_hbm, weights_hbm, prop_ref,
    out_ref,
    field_ref, brick_ref, index_ref, count_ref, weights_ref, out_r,
    prop, step_prop, rows_f, packed, recv, mixw, angles,
    fpeer_s, fpeer_r, fhalo_s, fhalo_r,
    apeer_s, apeer_r, ahalo_s, ahalo_r,
    sines, cosines, state, out_s,
    load_sem, prop_sem, pp_ss, pp_rs, a2a_ss, a2a_rs, fp_sem, fh_ss, fh_rs, ap_ss, ap_rs, ah_ss, ah_rs, out_sem,
):
    i = lax.axis_index("az")
    j = lax.axis_index("dep")
    other = 1 - j
    h = lax.rem(i + j + 1, 2)
    first = h == 0
    rows = 2 * half
    whole = prop.shape[2]
    block_rows = LANES
    share = lax.rem(i, 2)
    twin = i + 1 - 2 * share
    window = half + 2 * halo
    wide = half + 2 * halo
    shift = rows - wide
    chunks = packed.shape[0]
    depth = brick_ref.shape[1]
    bcol = brick_ref.shape[0]
    before = lax.rem(i + n - 1, n)
    after = lax.rem(i + 1, n)
    after_dep = lax.rem(i, 2)
    before_dep = 1 - after_dep

    barrier = pltpu.get_barrier_semaphore()

    def greet(q, carry):
        pl.semaphore_signal(
            barrier, inc=1, device_id=(lax.rem(i + 1 + q, n), j), device_id_type=MESH
        )
        return carry

    lax.fori_loop(0, n - 1, greet, 0)
    for target in (i, before, after):
        pl.semaphore_signal(barrier, inc=1, device_id=(target, other), device_id_type=MESH)

    loads = []
    for q, (src, dst) in enumerate(
        (
            (index_hbm, index_ref),
            (count_hbm, count_ref),
            (brick_hbm, brick_ref),
            (field_hbm, field_ref),
            (weights_hbm, weights_ref),
        )
    ):
        load = pltpu.make_async_copy(src, dst, load_sem.at[q])
        load.start()
        loads.append(load)
    fetches = []
    for f in range(factors):
        fetch = pltpu.make_async_copy(prop_ref.at[f], prop.at[f], prop_sem.at[f])
        fetch.start()
        fetches.append(fetch)

    for load in loads[0:3]:
        load.wait()
    slots = lax.broadcasted_iota(jnp.int32, (cap, n), 0)
    chosen = jnp.transpose(index_ref[0], (1, 0))
    chosen = jnp.where(slots < count_ref[...], chosen, -1)
    column = lax.broadcasted_iota(jnp.int32, (cap, bcol), 1)
    brick = brick_ref[...]
    group = min(n, 8)
    for g in range(n // group):
        onehot = jnp.concatenate(
            [
                (column == chosen[:, d : d + 1]).astype(jnp.float32).astype(jnp.bfloat16)
                for d in range(g * group, (g + 1) * group)
            ],
            axis=0,
        )
        picked = jnp.dot(onehot, brick, preferred_element_type=jnp.float32).astype(jnp.bfloat16)
        for c in range(chunks):
            packed[c, g * group : (g + 1) * group] = picked[
                :, c * LANES : (c + 1) * LANES
            ].reshape(group, cap, LANES)

    pl.semaphore_wait(barrier, n + 2)

    planes = 4 if n % 4 == 0 else 1
    plane = n // planes
    mine = lax.div(i, plane)
    spot = lax.rem(i, plane)
    if planes == 4:
        upper = lax.div(mine, 2)
        order = (3 - 3 * upper, 2 - upper, mine + 1 - 2 * lax.rem(mine, 2), mine)
    else:
        order = (mine,)

    def send(c, target):
        pltpu.make_async_remote_copy(
            src_ref=packed.at[c, target],
            dst_ref=recv.at[c, i],
            send_sem=a2a_ss.at[c],
            recv_sem=a2a_rs.at[c],
            device_id=(target, j),
            device_id_type=MESH,
        ).start()

    for c in range(chunks):

        @pl.when(i != n - 1)
        def _():
            for ahead in (2 * c, 2 * c + 1):
                if ahead < chunks:
                    send(ahead, n - 1)

        for p, there in enumerate(order):
            own = p == planes - 1

            def spread(q, carry, there=there, own=own):
                target = there * plane + lax.rem(spot + q + own, plane)

                @pl.when(target != n - 1)
                def _():
                    send(c, target)

                return carry

            lax.fori_loop(0, plane - own, spread, 0)
        recv[c, i] = packed[c, i]

    loads[3].wait()

    def strided(ref, start, stride):
        return jnp.concatenate(
            [ref[c, pl.ds(start, rows, stride=stride), :] for c in range(ref.shape[0])], axis=1
        )

    def field_part(p):
        return jnp.concatenate(
            [
                field_ref[pl.ds(2 * c + p, rows, stride=2 * chunks), :]
                for c in range(chunks)
            ],
            axis=1,
        )

    parts = [field_part(p) for p in range(2)]
    for p in range(2):
        x = parts[p]
        fpeer_s[p] = jnp.where(first, x[shift:rows], x[0:wide]).astype(jnp.bfloat16)
    fhalo_s[0] = jnp.concatenate([parts[0][0:halo], parts[1][0:halo]], axis=0).astype(jnp.bfloat16)
    fhalo_s[1] = jnp.concatenate(
        [parts[0][rows - halo : rows], parts[1][rows - halo : rows]], axis=0
    ).astype(jnp.bfloat16)

    def remote(src, dst, send_sem, recv_sem, target):
        return pltpu.make_async_remote_copy(
            src_ref=src, dst_ref=dst, send_sem=send_sem, recv_sem=recv_sem,
            device_id=target, device_id_type=MESH,
        )

    def local_wait(ref, sem):
        pltpu.make_async_copy(ref, ref, sem).wait()

    pending = []
    copy = remote(fpeer_s, fpeer_r, fp_sem.at[0], fp_sem.at[1], (i, other))
    copy.start()
    pending.append((fpeer_s, fp_sem.at[0]))
    remote(fhalo_s.at[0], fhalo_r.at[j], fh_ss.at[0], fh_rs.at[j], (before, before_dep)).start()
    remote(fhalo_s.at[1], fhalo_r.at[j], fh_ss.at[1], fh_rs.at[j], (after, after_dep)).start()
    pending.append((fhalo_s.at[0], fh_ss.at[0]))
    pending.append((fhalo_s.at[1], fh_ss.at[1]))

    loads[4].wait()
    for a in range(rows):
        block = weights_ref[a].astype(jnp.float32)
        for c in range(n * cap // LANES):
            rows_f[c, steps * a : steps * (a + 1), :] = block[:, c * LANES : (c + 1) * LANES]
    for k in range(steps):
        mixw[k * rows : (k + 1) * rows, :] = strided(rows_f, k, steps).astype(jnp.bfloat16)

    def windowed(body, edge, low):
        return jnp.where(
            first,
            jnp.concatenate([edge, body[0 : half + halo]], axis=0),
            jnp.concatenate([body[low : low + half + halo], edge], axis=0),
        )

    def finish(c):
        cols = pl.ds(c * LANES, LANES)
        local_wait(apeer_r.at[c], ap_rs.at[c])
        for side in range(2):
            local_wait(ahalo_r.at[c, side], ah_rs.at[c, side])
        edge_own = ahalo_r[c, j].astype(jnp.float32)
        edge_other = ahalo_r[c, other].astype(jnp.float32)
        for k in range(steps):
            own = windowed(
                angles[c, k * rows : (k + 1) * rows, :],
                edge_own[k * halo : (k + 1) * halo],
                rows - half - halo,
            )
            s, co = sine_cosine(own)
            sines[k, j, :, cols] = s
            cosines[k, j, :, cols] = co
            far = windowed(
                apeer_r[c, k].astype(jnp.float32),
                edge_other[k * halo : (k + 1) * halo],
                wide - half - halo,
            )
            s, co = sine_cosine(far)
            sines[k, other, :, cols] = s
            cosines[k, other, :, cols] = co

    def operand(re, im):
        re = re.astype(jnp.bfloat16)
        im = im.astype(jnp.bfloat16)
        left = jnp.concatenate([re, im], axis=0)
        right = jnp.concatenate([-im, re], axis=0)
        return jnp.concatenate([left, right], axis=1)

    def compose(b):
        at = pl.multiple_of(share * (whole // 2) + b * block_rows, block_rows)
        span = pl.ds(at, block_rows)
        re = prop[0, span, :]
        im = prop[0, pl.ds(whole + at, block_rows), :]
        for f in range(1, factors):
            mixed = jnp.dot(operand(re, im), prop[f], preferred_element_type=jnp.float32)
            re, im = mixed[0:block_rows], mixed[block_rows : 2 * block_rows]
        step_prop[0, span, :] = re.astype(jnp.bfloat16)
        step_prop[1, span, :] = im.astype(jnp.bfloat16)
        piece = step_prop.at[:, span, :]
        remote(piece, piece, pp_ss.at[b], pp_rs.at[b], (twin, j)).start()
        pending.append((piece, pp_ss.at[b]))

    for fetch in fetches:
        fetch.wait()
    blocks = pp_ss.shape[0]
    for c in range(chunks):
        for b in range(min(c * blocks // 2, blocks), min((c + 1) * blocks // 2, blocks)):
            compose(b)
        local_wait(recv.at[c, pl.ds(0, n - 1)], a2a_rs.at[c])
        flat = recv[c].reshape(n * cap, LANES)
        speed = jnp.dot(mixw[...], flat, preferred_element_type=jnp.float32)
        angle = -angle_rate * speed
        angles[c] = angle
        heads, tails = [], []
        for k in range(steps):
            x = angle[k * rows : (k + 1) * rows]
            apeer_s[c, k] = jnp.where(first, x[shift:rows], x[0:wide]).astype(jnp.bfloat16)
            heads.append(x[0:halo])
            tails.append(x[rows - halo : rows])
        ahalo_s[c, 0] = jnp.concatenate(heads, axis=0).astype(jnp.bfloat16)
        ahalo_s[c, 1] = jnp.concatenate(tails, axis=0).astype(jnp.bfloat16)
        remote(
            ahalo_s.at[c, 0], ahalo_r.at[c, j], ah_ss.at[c, 0], ah_rs.at[c, j],
            (before, before_dep),
        ).start()
        remote(
            ahalo_s.at[c, 1], ahalo_r.at[c, j], ah_ss.at[c, 1], ah_rs.at[c, j],
            (after, after_dep),
        ).start()
        remote(apeer_s.at[c], apeer_r.at[c], ap_ss.at[c], ap_rs.at[c], (i, other)).start()
        pending.append((ahalo_s.at[c, 0], ah_ss.at[c, 0]))
        pending.append((ahalo_s.at[c, 1], ah_ss.at[c, 1]))
        pending.append((apeer_s.at[c], ap_ss.at[c]))
    local_wait(fpeer_r, fp_sem.at[1])
    for side in range(2):
        local_wait(fhalo_r.at[side], fh_rs.at[side])
    edges = [fhalo_r[j].astype(jnp.float32), fhalo_r[other].astype(jnp.float32)]
    for p in range(2):
        part = field_part(p).astype(jnp.bfloat16).astype(jnp.float32)
        state[p, j] = windowed(
            part, edges[0][p * halo : (p + 1) * halo], rows - half - halo
        )
        state[p, other] = windowed(
            fpeer_r[p].astype(jnp.float32),
            edges[1][p * halo : (p + 1) * halo],
            wide - half - halo,
        )
    for c in range(chunks):
        finish(c)
    for b in range(blocks):
        at = pl.multiple_of((1 - share) * (whole // 2) + b * block_rows, block_rows)
        local_wait(step_prop.at[:, pl.ds(at, block_rows), :], pp_rs.at[b])
    def laplace(x):
        one = pltpu.roll(x, 1, 0) + pltpu.roll(x, window - 1, 0)
        two = pltpu.roll(x, 2, 0) + pltpu.roll(x, window - 2, 0)
        return (16.0 * one - 30.0 * x - two) * (1.0 / 12.0)

    def couple(k):
        tops, lows = [], []
        for side in range(2):
            re, im = state[0, side], state[1, side]
            co, si = cosines[k, side], sines[k, side]
            sre = re * co - im * si
            sim = re * si + im * co
            lre, lim = laplace(sre), laplace(sim)
            tops.append(sre + couple_real * lre - couple_imag * lim)
            lows.append(sim + couple_real * lim + couple_imag * lre)
        return jnp.concatenate(tops, axis=1), jnp.concatenate(lows, axis=1)

    def march(k, carry):
        re, im = couple(k)
        mixed = jnp.dot(operand(re, im), step_prop[...].reshape(2 * whole, whole), preferred_element_type=jnp.float32)
        re, im = mixed[0:window], mixed[window : 2 * window]
        for side in range(2):
            state[0, side] = re[:, side * depth : (side + 1) * depth]
            state[1, side] = im[:, side * depth : (side + 1) * depth]
        return carry

    lax.fori_loop(0, steps - 1, march, 0)

    def put(block, p, x):
        start = block * (half * 2 * chunks)
        for c in range(chunks):
            out_ref[pl.ds(start + 2 * c + p, half, stride=2 * chunks), :] = x[
                :, c * LANES : (c + 1) * LANES
            ]

    re, im = couple(steps - 1)
    both = operand(re, im)

    def last(side):
        columns = pl.ds(pl.multiple_of(side * depth, LANES), depth)
        mixed = jnp.dot(
            both, step_prop[:, :, columns].reshape(2 * whole, depth), preferred_element_type=jnp.float32
        )
        return [mixed[p * window + halo : p * window + halo + half] for p in range(2)]

    ready = last(other)
    for p in range(2):
        out_s[p] = ready[p].astype(jnp.bfloat16)
    remote(out_s, out_r, out_sem.at[0], out_sem.at[1], (i, other)).start()
    ready = last(j)
    for p in range(2):
        put(h, p, ready[p])

    for c in range(chunks):
        local_wait(packed.at[c, pl.ds(0, n - 1)], a2a_ss.at[c])
    for ref, sem in pending:
        local_wait(ref, sem)
    local_wait(out_s, out_sem.at[0])
    local_wait(out_r, out_sem.at[1])
    for p in range(2):
        put(1 - h, p, out_r[p].astype(jnp.float32))


def per_device(field, brick_speed, send_index, send_count, weights, propagator):
    n = lax.axis_size("az")
    rows, _, depth = field.shape
    steps = weights.shape[1]
    factors, _, whole, _ = propagator.shape
    cap = send_index.shape[2]
    half = rows // 2
    halo = 2 * steps
    window = half + 2 * halo
    wide = half + 2 * halo
    chunks = depth // LANES
    merged = propagator.reshape(factors, 2 * whole, whole)
    flat_field = field.reshape(rows, 2, chunks, LANES).transpose(0, 2, 1, 3).reshape(-1, LANES)
    bf16, f32 = jnp.bfloat16, jnp.float32
    dma = pltpu.SemaphoreType.DMA
    vmem = pl.BlockSpec(memory_space=pltpu.VMEM)
    out = pl.pallas_call(
        functools.partial(march_kernel, n, steps, factors, cap, halo, half),
        out_shape=pltpu.VMEM(flat_field.shape, f32),
        in_specs=[pl.BlockSpec(memory_space=pl.ANY)] * 6,
        out_specs=vmem,
        scratch_shapes=[
            pltpu.VMEM(flat_field.shape, f32),
            pltpu.VMEM(brick_speed.shape, bf16),
            pltpu.VMEM(send_index.shape, jnp.int32),
            pltpu.VMEM(send_count.shape, jnp.int32),
            pltpu.VMEM(weights.shape, bf16),
            pltpu.VMEM((2, half, depth), bf16),
            pltpu.VMEM((factors, 2 * whole, whole), bf16),
            pltpu.VMEM((2, whole, whole), bf16),
            pltpu.VMEM((n * cap // LANES, rows * steps, LANES), f32),
            pltpu.VMEM((chunks, n, cap, LANES), bf16),
            pltpu.VMEM((chunks, n, cap, LANES), bf16),
            pltpu.VMEM((rows * steps, n * cap), bf16),
            pltpu.VMEM((chunks, rows * steps, LANES), f32),
            pltpu.VMEM((2, wide, depth), bf16),
            pltpu.VMEM((2, wide, depth), bf16),
            pltpu.VMEM((2, 2 * halo, depth), bf16),
            pltpu.VMEM((2, 2 * halo, depth), bf16),
            pltpu.VMEM((chunks, steps, wide, LANES), bf16),
            pltpu.VMEM((chunks, steps, wide, LANES), bf16),
            pltpu.VMEM((chunks, 2, steps * halo, LANES), bf16),
            pltpu.VMEM((chunks, 2, steps * halo, LANES), bf16),
            pltpu.VMEM((steps, 2, window, depth), f32),
            pltpu.VMEM((steps, 2, window, depth), f32),
            pltpu.VMEM((2, 2, window, depth), f32),
            pltpu.VMEM((2, half, depth), bf16),
            dma((5,)),
            dma((factors,)),
            dma((whole // 2 // LANES,)),
            dma((whole // 2 // LANES,)),
            dma((chunks,)),
            dma((chunks,)),
            dma((2,)),
            dma((2,)),
            dma((2,)),
            dma((chunks,)),
            dma((chunks,)),
            dma((chunks, 2)),
            dma((chunks, 2)),
            dma((2,)),
        ],
        compiler_params=pltpu.CompilerParams(collective_id=0, has_side_effects=True),
    )(flat_field, brick_speed, send_index, send_count, weights, merged)
    return out.reshape(rows, chunks, 2, LANES).transpose(0, 2, 1, 3).reshape(rows, 2, depth)


def solution(mesh):
    placed = (
        P("az", None, "dep"),
        P("az", "dep"),
        P("az", None, None),
        P("az", None),
        P("az", None, None),
        P(),
    )
    return jax.shard_map(
        per_device, mesh=mesh, in_specs=placed, out_specs=P("az", None, "dep"), check_vma=False
    )
```

```python
import functools
import math

import jax
import jax.numpy as jnp
from jax import lax
from jax.experimental import pallas as pl
from jax.experimental.pallas import tpu as pltpu
from jax.sharding import PartitionSpec as P

angle_rate = 200.0 / 1500.0
couple_real = 0.1
couple_imag = 0.15
MESH = pl.DeviceIdType.MESH
LANES = 128


def sine_cosine(x):
    turns = jnp.floor(x * (2.0 / math.pi) + 0.5)
    r = x - turns * 1.5703125
    r = r - turns * 4.837512969970703125e-4
    r = r - turns * 7.549789948768648e-8
    quadrant = turns.astype(jnp.int32)
    r2 = r * r
    sine = r + r * r2 * (-1.0 / 6.0 + r2 * (1.0 / 120.0 + r2 * (-1.0 / 5040.0)))
    cosine = 1.0 + r2 * (-0.5 + r2 * (1.0 / 24.0 + r2 * (-1.0 / 720.0 + r2 * (1.0 / 40320.0))))
    swap = (quadrant & 1) == 1
    out_sine = jnp.where(swap, cosine, sine)
    out_cosine = jnp.where(swap, sine, cosine)
    out_sine = jnp.where((quadrant & 2) == 2, -out_sine, out_sine)
    out_cosine = jnp.where(((quadrant + 1) & 2) == 2, -out_cosine, out_cosine)
    return out_sine, out_cosine


def march_kernel(
    n, steps, factors, cap, halo,
    field_hbm, brick_hbm, index_hbm, count_hbm, weights_hbm, prop_ref,
    out_ref,
    field_ref, brick_ref, index_ref, count_ref, weights_ref,
    prop, step_prop, rows_f, picks, packed, recv, mixw, angles,
    fpeer_s, fpeer_r, fhalo_s, fhalo_r,
    apeer_s, apeer_r, ahalo_s, ahalo_r,
    sines, cosines, state, stencil,
    load_sem, brick_sem, prop_sem, pp_ss, pp_rs, a2a_ss, a2a_rs, fp_sem, fh_ss, fh_rs, ap_ss, ap_rs, ah_ss, ah_rs,
):
    i = lax.axis_index("az")
    j = lax.axis_index("dep")
    other = 1 - j
    rows = weights_ref.shape[0]
    whole = prop.shape[2]
    block_rows = LANES
    share = lax.rem(i, 2)
    twin = i + 1 - 2 * share
    window = rows + 2 * halo
    chunks = packed.shape[0]
    depth = chunks * LANES
    bcol = brick_ref.shape[1]
    before = lax.rem(i + n - 1, n)
    after = lax.rem(i + 1, n)
    deps = (j, other)

    barrier = pltpu.get_barrier_semaphore()

    loads = []

    def load(src, dst):
        copy = pltpu.make_async_copy(src, dst, load_sem.at[len(loads)])
        copy.start()
        loads.append(copy)

    load(index_hbm, index_ref)
    load(count_hbm, count_ref)
    bricks = []
    for c in range(chunks):
        copy = pltpu.make_async_copy(
            brick_hbm.at[:, pl.ds(c * LANES, LANES)], brick_ref.at[c], brick_sem.at[c]
        )
        copy.start()
        bricks.append(copy)

    def greet(q, carry):
        pl.semaphore_signal(
            barrier, inc=1, device_id=(lax.rem(i + 1 + q, n), j), device_id_type=MESH
        )
        return carry

    lax.fori_loop(0, n - 1, greet, 0)
    for target in (i, before, after):
        pl.semaphore_signal(barrier, inc=1, device_id=(target, other), device_id_type=MESH)

    load(field_hbm, field_ref)
    load(weights_hbm, weights_ref)
    fetches = []
    for f in range(factors):
        fetch = pltpu.make_async_copy(prop_ref.at[f], prop.at[f], prop_sem.at[f])
        fetch.start()
        fetches.append(fetch)

    for copy in loads[0:2]:
        copy.wait()
    slots = lax.broadcasted_iota(jnp.int32, (cap, n), 0)
    chosen = jnp.transpose(index_ref[0], (1, 0))
    chosen = jnp.where(slots < count_ref[...], chosen, -1)
    column = lax.broadcasted_iota(jnp.int32, (cap, bcol), 1)
    group = min(n, 8)
    for d in range(n):
        picks[d * cap : (d + 1) * cap, :] = (
            (column == chosen[:, d : d + 1]).astype(jnp.float32).astype(jnp.bfloat16)
        )

    def pick(c):
        bricks[c].wait()
        for g in range(n // group):
            picked = jnp.dot(
                picks[g * group * cap : (g + 1) * group * cap, :], brick_ref[c],
                preferred_element_type=jnp.float32,
            )
            packed[c, g * group : (g + 1) * group] = picked.astype(jnp.bfloat16).reshape(
                group, cap, LANES
            )

    pick(0)
    pl.semaphore_wait(barrier, n + 2)

    planes = 4 if n % 4 == 0 else 1
    plane = n // planes
    mine = lax.div(i, plane)
    spot = lax.rem(i, plane)
    if planes == 4:
        upper = lax.div(mine, 2)
        order = (3 - 3 * upper, 2 - upper, mine + 1 - 2 * lax.rem(mine, 2), mine)
    else:
        order = (mine,)

    def send(c, target):
        pltpu.make_async_remote_copy(
            src_ref=packed.at[c, target],
            dst_ref=recv.at[c, i],
            send_sem=a2a_ss.at[0],
            recv_sem=a2a_rs.at[c],
            device_id=(target, j),
            device_id_type=MESH,
        ).start()

    def send_last(c):
        @pl.when(i != n - 1)
        def _():
            send(c, n - 1)

    def send_all(c):
        for p, there in enumerate(order):
            own = p == planes - 1

            def spread(q, carry, there=there, own=own):
                target = there * plane + lax.rem(spot + q + own, plane)

                @pl.when(target != n - 1)
                def _():
                    send(c, target)

                return carry

            lax.fori_loop(0, plane - own, spread, 0)

    send_last(0)
    send_all(0)
    for c in range(1, chunks):
        for ahead in (2 * c - 1, 2 * c):
            if ahead < chunks:
                pick(ahead)
                send_last(ahead)
        send_all(c)
    for c in range(chunks):
        recv[c, i] = packed[c, i]

    loads[2].wait()

    def strided(ref, start, stride):
        return jnp.concatenate(
            [ref[c, pl.ds(start, rows, stride=stride), :] for c in range(ref.shape[0])], axis=1
        )

    def field_part(p):
        return jnp.concatenate(
            [
                field_ref[pl.ds(2 * c + p, rows, stride=2 * chunks), :]
                for c in range(chunks)
            ],
            axis=1,
        )

    parts = [field_part(p) for p in range(2)]
    for p in range(2):
        fpeer_s[p] = parts[p].astype(jnp.bfloat16)
    fhalo_s[0] = jnp.concatenate([parts[0][0:halo], parts[1][0:halo]], axis=0).astype(jnp.bfloat16)
    fhalo_s[1] = jnp.concatenate(
        [parts[0][rows - halo : rows], parts[1][rows - halo : rows]], axis=0
    ).astype(jnp.bfloat16)

    def remote(src, dst, send_sem, recv_sem, target):
        return pltpu.make_async_remote_copy(
            src_ref=src, dst_ref=dst, send_sem=send_sem, recv_sem=recv_sem,
            device_id=target, device_id_type=MESH,
        )

    def local_wait(ref, sem):
        pltpu.make_async_copy(ref, ref, sem).wait()

    def launch(src, dst, send_sem, recv_sem, target):
        remote(src, dst, send_sem, recv_sem, target).start()

    launch(fpeer_s, fpeer_r, fp_sem.at[0], fp_sem.at[1], (i, other))
    for t, dep in enumerate(deps):
        launch(fhalo_s.at[0], fhalo_r.at[1, j], fh_ss.at[t], fh_rs.at[0], (before, dep))
        launch(fhalo_s.at[1], fhalo_r.at[0, j], fh_ss.at[t], fh_rs.at[0], (after, dep))

    loads[3].wait()
    for a in range(rows):
        block = weights_ref[a].astype(jnp.float32)
        for c in range(n * cap // LANES):
            rows_f[c, steps * a : steps * (a + 1), :] = block[:, c * LANES : (c + 1) * LANES]
    for k in range(steps):
        mixw[k * rows : (k + 1) * rows, :] = strided(rows_f, k, steps).astype(jnp.bfloat16)

    def windowed(low, body, high):
        return jnp.concatenate([low, body, high], axis=0)

    def finish(c, k):
        cols = pl.ds(c * LANES, LANES)
        for side in deps:
            body = angles[c, k] if side is j else apeer_r[c, k].astype(jnp.float32)
            low = ahalo_r[c, 0, side, k].astype(jnp.float32)
            high = ahalo_r[c, 1, side, k].astype(jnp.float32)
            s, co = sine_cosine(windowed(low, body, high))
            sines[k, side, :, cols] = s
            cosines[k, side, :, cols] = co

    def operand(re, im):
        re = re.astype(jnp.bfloat16)
        im = im.astype(jnp.bfloat16)
        left = jnp.concatenate([re, im], axis=0)
        right = jnp.concatenate([-im, re], axis=0)
        return jnp.concatenate([left, right], axis=1)

    def compose(b):
        at = pl.multiple_of(share * (whole // 2) + b * block_rows, block_rows)
        span = pl.ds(at, block_rows)
        re = prop[0, span, :]
        im = prop[0, pl.ds(whole + at, block_rows), :]
        for f in range(1, factors):
            mixed = jnp.dot(operand(re, im), prop[f], preferred_element_type=jnp.float32)
            re, im = mixed[0:block_rows], mixed[block_rows : 2 * block_rows]
        step_prop[0, span, :] = re.astype(jnp.bfloat16)
        step_prop[1, span, :] = im.astype(jnp.bfloat16)
        piece = step_prop.at[:, span, :]
        remote(piece, piece, pp_ss.at[0], pp_rs.at[0], (twin, j)).start()

    for fetch in fetches:
        fetch.wait()
    blocks = whole // 2 // LANES
    early = max(chunks - 2, 0)
    for c in range(chunks):
        for b in range(min(c * blocks // 2, blocks), min((c + 1) * blocks // 2, blocks)):
            compose(b)
        local_wait(recv.at[c, pl.ds(0, n - 1)], a2a_rs.at[c])
        flat = recv[c].reshape(n * cap, LANES)
        speed = jnp.dot(mixw[...], flat, preferred_element_type=jnp.float32)
        angle = -angle_rate * speed
        for k in range(steps):
            x = angle[k * rows : (k + 1) * rows]
            angles[c, k] = x
            apeer_s[c, k] = x.astype(jnp.bfloat16)
            ahalo_s[c, 0, k] = x[0:halo].astype(jnp.bfloat16)
            ahalo_s[c, 1, k] = x[rows - halo : rows].astype(jnp.bfloat16)
        group = int(c >= early)

        def exchange_edges():
            for t, dep in enumerate(deps):
                launch(
                    ahalo_s.at[c, 0], ahalo_r.at[c, 1, j], ah_ss.at[t], ah_rs.at[group],
                    (before, dep),
                )
                launch(
                    ahalo_s.at[c, 1], ahalo_r.at[c, 0, j], ah_ss.at[t], ah_rs.at[group],
                    (after, dep),
                )

        if c < early:
            wanted = [(c, k) for k in range(steps)]
        elif c < chunks - 1:
            wanted = [(c, k) for k in range(steps // 2)]
        else:
            wanted = [
                (b, k) for k in range(steps) for b in range(early, chunks)
                if b == c or k >= steps // 2
            ]
        for q, (b, k) in enumerate(wanted):
            launch(
                apeer_s.at[b, k], apeer_r.at[b, k], ap_ss.at[0],
                ap_rs.at[0 if b < early else 1 + k], (i, other),
            )
            if q == 0:
                exchange_edges()
    local_wait(fpeer_r, fp_sem.at[1])
    local_wait(fhalo_r, fh_rs.at[0])
    for side in deps:
        lows = fhalo_r[0, side].astype(jnp.float32)
        highs = fhalo_r[1, side].astype(jnp.float32)
        for p in range(2):
            if side is j:
                part = field_part(p).astype(jnp.bfloat16).astype(jnp.float32)
            else:
                part = fpeer_r[p].astype(jnp.float32)
            span = slice(p * halo, (p + 1) * halo)
            state[p, side] = windowed(lows[span], part, highs[span])
    if early:
        local_wait(apeer_r.at[pl.ds(0, early)], ap_rs.at[0])
        local_wait(ahalo_r.at[pl.ds(0, early)], ah_rs.at[0])
    for c in range(early):
        for k in range(steps):
            finish(c, k)
    local_wait(ahalo_r.at[pl.ds(early, chunks - early)], ah_rs.at[1])

    def arrive(k):
        local_wait(apeer_r.at[pl.ds(early, chunks - early), k], ap_rs.at[1 + k])

    def settle(k):
        for c in range(early, chunks):
            finish(c, k)

    def half_prop(which):
        at = pl.multiple_of(which * (whole // 2), LANES)
        return step_prop.at[:, pl.ds(at, whole // 2), :]

    local_wait(half_prop(1 - share), pp_rs.at[0])
    across = lax.broadcasted_iota(jnp.int32, (window, window), 0)
    gap = across - lax.broadcasted_iota(jnp.int32, (window, window), 1)
    near = jnp.where((gap == 1) | (gap == -1), 16.0, jnp.where((gap == 2) | (gap == -2), -1.0, 0.0))
    stencil[...] = jnp.where(gap == 0, -30.0, near).astype(jnp.bfloat16)

    def laplace(x):
        return jnp.dot(stencil[...], x.astype(jnp.bfloat16), preferred_element_type=jnp.float32)

    def couple(k):
        tops, lows = [], []
        for side in range(2):
            re, im = state[0, side], state[1, side]
            co, si = cosines[k, side], sines[k, side]
            sre = re * co - im * si
            sim = re * si + im * co
            lre, lim = laplace(sre), laplace(sim)
            tops.append(sre + (couple_real / 12.0) * lre - (couple_imag / 12.0) * lim)
            lows.append(sim + (couple_real / 12.0) * lim + (couple_imag / 12.0) * lre)
        return jnp.concatenate(tops, axis=1), jnp.concatenate(lows, axis=1)

    def march(k, carry):
        re, im = couple(k)
        both = operand(re, im)
        arrive(k + 1)
        mixed = jnp.dot(both, step_prop[...].reshape(2 * whole, whole), preferred_element_type=jnp.float32)
        settle(k + 1)
        re, im = mixed[0:window], mixed[window : 2 * window]
        for side in range(2):
            state[0, side] = re[:, side * depth : (side + 1) * depth]
            state[1, side] = im[:, side * depth : (side + 1) * depth]
        return carry

    arrive(0)
    settle(0)
    lax.fori_loop(0, steps - 1, march, 0)

    re, im = couple(steps - 1)
    inner = slice(halo, halo + rows)
    both = operand(re[inner], im[inner])
    columns = pl.ds(pl.multiple_of(j * depth, LANES), depth)
    mixed = jnp.dot(
        both, step_prop[:, :, columns].reshape(2 * whole, depth), preferred_element_type=jnp.float32
    )
    for p in range(2):
        for c in range(chunks):
            out_ref[pl.ds(2 * c + p, rows, stride=2 * chunks), :] = mixed[
                p * rows : (p + 1) * rows, c * LANES : (c + 1) * LANES
            ]

    local_wait(packed.at[:, pl.ds(0, n - 1)], a2a_ss.at[0])
    local_wait(fpeer_s, fp_sem.at[0])
    local_wait(half_prop(share), pp_ss.at[0])
    local_wait(apeer_s, ap_ss.at[0])
    for t in range(2):
        local_wait(fhalo_s, fh_ss.at[t])
        local_wait(ahalo_s, ah_ss.at[t])


def per_device(field, brick_speed, send_index, send_count, weights, propagator):
    n = lax.axis_size("az")
    rows, _, depth = field.shape
    steps = weights.shape[1]
    factors, _, whole, _ = propagator.shape
    cap = send_index.shape[2]
    halo = 2 * steps
    window = rows + 2 * halo
    chunks = depth // LANES
    merged = propagator.reshape(factors, 2 * whole, whole)
    flat_field = field.reshape(rows, 2, chunks, LANES).transpose(0, 2, 1, 3).reshape(-1, LANES)
    bf16, f32 = jnp.bfloat16, jnp.float32
    dma = pltpu.SemaphoreType.DMA
    vmem = pl.BlockSpec(memory_space=pltpu.VMEM)
    out = pl.pallas_call(
        functools.partial(march_kernel, n, steps, factors, cap, halo),
        out_shape=pltpu.VMEM(flat_field.shape, f32),
        in_specs=[pl.BlockSpec(memory_space=pl.ANY)] * 6,
        out_specs=vmem,
        scratch_shapes=[
            pltpu.VMEM(flat_field.shape, f32),
            pltpu.VMEM((chunks, brick_speed.shape[0], LANES), bf16),
            pltpu.VMEM(send_index.shape, jnp.int32),
            pltpu.VMEM(send_count.shape, jnp.int32),
            pltpu.VMEM(weights.shape, bf16),
            pltpu.VMEM((factors, 2 * whole, whole), bf16),
            pltpu.VMEM((2, whole, whole), bf16),
            pltpu.VMEM((n * cap // LANES, rows * steps, LANES), f32),
            pltpu.VMEM((n * cap, brick_speed.shape[0]), bf16),
            pltpu.VMEM((chunks, n, cap, LANES), bf16),
            pltpu.VMEM((chunks, n, cap, LANES), bf16),
            pltpu.VMEM((rows * steps, n * cap), bf16),
            pltpu.VMEM((chunks, steps, rows, LANES), f32),
            pltpu.VMEM((2, rows, depth), bf16),
            pltpu.VMEM((2, rows, depth), bf16),
            pltpu.VMEM((2, 2 * halo, depth), bf16),
            pltpu.VMEM((2, 2, 2 * halo, depth), bf16),
            pltpu.VMEM((chunks, steps, rows, LANES), bf16),
            pltpu.VMEM((chunks, steps, rows, LANES), bf16),
            pltpu.VMEM((chunks, 2, steps, halo, LANES), bf16),
            pltpu.VMEM((chunks, 2, 2, steps, halo, LANES), bf16),
            pltpu.VMEM((steps, 2, window, depth), f32),
            pltpu.VMEM((steps, 2, window, depth), f32),
            pltpu.VMEM((2, 2, window, depth), f32),
            pltpu.VMEM((window, window), bf16),
            dma((4,)),
            dma((chunks,)),
            dma((factors,)),
            dma((1,)),
            dma((1,)),
            dma((1,)),
            dma((chunks,)),
            dma((2,)),
            dma((2,)),
            dma((1,)),
            dma((1,)),
            dma((1 + steps,)),
            dma((2,)),
            dma((2,)),
        ],
        compiler_params=pltpu.CompilerParams(collective_id=0, has_side_effects=True),
    )(flat_field, brick_speed, send_index, send_count, weights, merged)
    return out.reshape(rows, chunks, 2, LANES).transpose(0, 2, 1, 3).reshape(rows, 2, depth)


def solution(mesh):
    placed = (
        P("az", None, "dep"),
        P("az", "dep"),
        P("az", None, None),
        P("az", None),
        P("az", None, None),
        P(),
    )
    return jax.shard_map(
        per_device, mesh=mesh, in_specs=placed, out_specs=P("az", None, "dep"), check_vma=False
    )
```
